32 devices in a mesh: dp: 4 (over y, core), expert: 8 (over z, x).
Axes of the slice: x: 2, y: 2, z: 4, core: 2. Of those that a mesh axis runs over, the one named last changes fastest.
Arguments:
- out_grad: bfloat16 [16384, 3584], P(('dp', 'expert')), may hold values from -6 to 6
- expert_ids: int32 [16384, 8], P(('dp', 'expert')), may hold values from 0 to 255, as said below
- affinity_logits: float32 [16384, 8], P(('dp', 'expert')), may hold values from -6 to 6
- activations: bfloat16 [4, 8, 256, 1024], P('dp', 'expert'), may hold values from -0.29882812 to 0.29882812
- down_weight: bfloat16 [8, 1024, 3584], P('expert', 'dp'), may hold values from -0.1875 to 0.1875
Outputs:
- hidden_grad: bfloat16 [4, 8, 256, 1024], P('dp', 'expert')
- weight_grad: float32 [8, 1024, 3584], P('expert', 'dp')
- logit_grad: float32 [16384, 8], P(('dp', 'expert'))
The draws below stay inside these ranges and needn't reach their ends.
Inputs may be any that keep to these rules, and one draw needn't show every extreme that they name: `expert_ids`: the k-th id of every token (k counted from 0) is congruent to k modulo 8. In every aligned block of 512 rows no id of the first column is named more than 32 times, and some multiple of 32 is named exactly 32 times.
All inputs are finite; a program needn't handle non-finite values.
Results may differ from the reference program's by a relative error of at most 0.012.
Values may be sent and summed in bfloat16 or wider, within the bound.
A program may use at most 128 MiB of HBM per device.

```python
import jax
import jax.numpy as jnp
from jax import lax

D = 3584
FF = 1024
EXPERTS = 256
TOP = 8
TOK_DEV = 512
CAP = 32
SLOTS = 256
GROUP = 32
TOKENS = 16384
N_DP = 4
N_EXPERT = 8


def block_ids(block_key):
    unit_count = EXPERTS // TOP
    stride = GROUP // TOP
    key_main, key_supply, key_order, key_rest = jax.random.split(block_key, 4)
    chosen = stride * jax.random.randint(key_main, (), 0, EXPERTS // GROUP)
    supply = jnp.arange((unit_count - 1) * CAP, dtype=jnp.int32) // CAP
    supply = supply + (supply >= chosen).astype(jnp.int32)
    supply = jax.random.permutation(key_supply, supply)[:TOK_DEV - CAP]
    leading = jnp.concatenate([jnp.full((CAP,), chosen, jnp.int32), supply.astype(jnp.int32)])
    leading = jax.random.permutation(key_order, leading)
    others = jax.random.randint(key_rest, (TOK_DEV, TOP - 1), 0, unit_count)
    chosen_units = jnp.concatenate([leading[:, None], others], axis=1)
    column_index = jnp.arange(TOP, dtype=jnp.int32)[None, :]
    return (column_index + TOP * chosen_units).astype(jnp.int32)


def draw_expert_ids(key, part):
    block_count = TOKENS // TOK_DEV
    block_keys = jax.random.split(jax.random.fold_in(key, 17), block_count)
    return jax.vmap(block_ids)(block_keys).reshape(TOKENS, TOP)


def block_scale(key, extent, shards, least, largest):
    def one(dim, blocks):
        steps = jax.random.uniform(jax.random.fold_in(jax.random.fold_in(key, 6), dim), (blocks,), jnp.float32, least / len(shards), largest / len(shards))
        return jnp.repeat(jnp.exp(steps), extent[dim] // blocks).reshape((-1,) + (1,) * (len(extent) - dim - 1))

    loudness = one(*shards[0])
    for cut in shards[1:]:
        loudness = loudness * one(*cut)
    return loudness


def scatter_about(key, extent, deviation, limit, cuts=(), held_as=jnp.bfloat16):
    loudness = block_scale(key, extent, cuts, -0.22, 0.18) if cuts else 1.0
    drawn = jax.random.normal(key, extent, jnp.float32) * deviation * loudness
    return jnp.minimum(jnp.maximum(drawn, -limit), limit).astype(held_as)


def setup_inputs(seed: int = 0) -> dict:
    seeds = jax.random.split(jax.random.key(seed), 6)
    out_grad = scatter_about(seeds[0], (TOKENS, D), 1.0, 6.0, ((0, 32),))
    expert_ids = draw_expert_ids(jax.random.fold_in(seeds[5], 71), 0)
    affinity_logits = scatter_about(seeds[2], (TOKENS, TOP), 1.5, 6.0, ((0, 32),), jnp.float32)
    activations = scatter_about(seeds[3], (N_DP, N_EXPERT, SLOTS, FF), 0.05, 0.29882812, ((0, 4), (1, 8)))
    down_weight = scatter_about(seeds[4], (N_EXPERT, FF, D), FF ** -0.5, 0.1875, ((0, 8), (1, 4)))
    return dict(out_grad=out_grad, expert_ids=expert_ids, affinity_logits=affinity_logits, activations=activations, down_weight=down_weight)


def expert_pass(operands):
    slot_rows, gate_slot, acts, weight = operands
    hidden_raw = jnp.dot(slot_rows, weight.T, preferred_element_type=jnp.float32)
    gate_col = gate_slot.astype(jnp.float32)[:, None]
    hidden_grad = (gate_col * hidden_raw).astype(jnp.bfloat16)
    slot_dgate = jnp.sum(hidden_raw * acts.astype(jnp.float32), axis=1)
    weighted = (gate_col * slot_rows.astype(jnp.float32)).astype(jnp.bfloat16)
    partial_grad = jnp.dot(acts.T, weighted, preferred_element_type=jnp.float32)
    partial_grad = lax.optimization_barrier(partial_grad.astype(jnp.bfloat16)).astype(jnp.float32)
    return hidden_grad, slot_dgate, partial_grad


def reference(out_grad, expert_ids, affinity_logits, activations, down_weight):
    rows_count = N_EXPERT * TOK_DEV

    def replica_step(accum, operands):
        grads, ident, logits, acts = operands
        affinity = jax.nn.sigmoid(logits)
        aff_total = jnp.sum(affinity, axis=1, keepdims=True)
        gate_vals = 2.5 * affinity / aff_total
        is_live = ident % GROUP == 0
        target = ident // GROUP
        experts_row = jnp.arange(N_EXPERT, dtype=jnp.int32)[None, None, :]
        onehot = ((target[:, :, None] == experts_row) & is_live[:, :, None]).astype(jnp.int32)
        per_token = jnp.sum(onehot, axis=1).reshape(N_EXPERT, TOK_DEV, N_EXPERT)
        before = (jnp.cumsum(per_token, axis=1) - per_token).reshape(rows_count, N_EXPERT)
        ranking = jnp.sum(onehot * before[:, None, :], axis=2)
        source_dev = (jnp.arange(rows_count, dtype=jnp.int32) // TOK_DEV)[:, None]
        slot_key = jnp.where(is_live, target * SLOTS + source_dev * CAP + ranking, N_EXPERT * SLOTS).reshape(-1).astype(jnp.int32)
        token_list = jnp.repeat(jnp.arange(rows_count, dtype=jnp.int32), TOP)
        token_of = jnp.full((N_EXPERT * SLOTS,), rows_count, jnp.int32).at[slot_key].set(token_list, mode="drop")
        gate_of = jnp.zeros((N_EXPERT * SLOTS,), jnp.float32).at[slot_key].set(gate_vals.reshape(-1), mode="drop")
        gate_of = gate_of.astype(jnp.bfloat16).reshape(N_EXPERT, SLOTS)
        padded = jnp.concatenate([grads, jnp.zeros((1, D), grads.dtype)], axis=0)
        slot_rows = padded[token_of].reshape(N_EXPERT, SLOTS, D)
        hidden_grad, slot_dgate, partial_grad = lax.map(expert_pass, (slot_rows, gate_of, acts, down_weight))
        flat_dgate = jnp.concatenate([slot_dgate.reshape(-1), jnp.zeros((1,), jnp.float32)])
        route_dgate = jnp.where(is_live, flat_dgate[slot_key].reshape(rows_count, TOP), jnp.zeros((), jnp.float32))
        mean_term = jnp.sum(route_dgate * affinity, axis=1, keepdims=True) / aff_total
        logit_grad = affinity * (1.0 - affinity) * (2.5 / aff_total) * (route_dgate - mean_term)
        return accum + partial_grad, (hidden_grad, logit_grad)

    operands = (out_grad.reshape(N_DP, rows_count, D), expert_ids.reshape(N_DP, rows_count, TOP),
                affinity_logits.reshape(N_DP, rows_count, TOP), activations)
    initial = jnp.zeros((N_EXPERT, FF, D), jnp.float32)
    weight_grad, (hidden_grad, logit_grad) = lax.scan(replica_step, initial, operands)
    return hidden_grad, weight_grad, logit_grad.reshape(TOKENS, TOP)
```

```python
import functools

import jax
import jax.numpy as jnp
from jax import lax
from jax.experimental import pallas as pl
from jax.experimental.pallas import tpu as pltpu
from jax.sharding import PartitionSpec as P

EXPERTS = 256
TOP = 8


def contract_rows(slot_rows, weight_rows):
    return lax.dot_general(
        slot_rows, weight_rows, (((1,), (1,)), ((), ())), preferred_element_type=jnp.float32
    )


def local_native(out_grad, expert_ids, affinity_logits, activations, down_weight):
    tok_rows = out_grad.shape[0]
    feat_width = out_grad.shape[1]
    peer_count = lax.axis_size("expert")
    capacity = tok_rows // 16
    slot_count = peer_count * capacity
    group_size = EXPERTS // peer_count
    affinity = jax.nn.sigmoid(affinity_logits)
    aff_total = jnp.sum(affinity, axis=1, keepdims=True)
    gate_vals = 2.5 * affinity / aff_total
    is_live = expert_ids % group_size == 0
    target = expert_ids // group_size
    experts_row = jnp.arange(peer_count, dtype=jnp.int32)[None, None, :]
    onehot = ((target[:, :, None] == experts_row) & is_live[:, :, None]).astype(jnp.int32)
    per_token = jnp.sum(onehot, axis=1)
    before = jnp.cumsum(per_token, axis=0) - per_token
    ranking = jnp.sum(onehot * before[:, None, :], axis=2)
    slot_key = jnp.where(is_live, target * capacity + ranking, slot_count).reshape(-1)
    token_list = jnp.repeat(jnp.arange(tok_rows, dtype=jnp.int32), TOP)
    source_of = (
        jnp.full((slot_count,), tok_rows, jnp.int32).at[slot_key].set(token_list, mode="drop")
    )
    gate_send = (
        jnp.zeros((slot_count,), jnp.float32).at[slot_key].set(gate_vals.reshape(-1), mode="drop")
    )
    gate_send = gate_send.astype(jnp.bfloat16).reshape(peer_count, capacity)
    padded = jnp.concatenate([out_grad, jnp.zeros((1, feat_width), out_grad.dtype)], axis=0)
    send_rows = padded[source_of].reshape(peer_count, capacity, feat_width)
    slot_rows, gate_in = (
        lax.all_to_all(send_rows, "expert", split_axis=0, concat_axis=0, tiled=True),
        lax.all_to_all(gate_send, "expert", split_axis=0, concat_axis=0, tiled=True),
    )
    slot_rows = slot_rows.reshape(slot_count, feat_width)
    gate_col = gate_in.reshape(slot_count, 1).astype(jnp.float32)
    hidden = activations.reshape(slot_count, activations.shape[-1])
    weight_shard = down_weight[0]
    gathered = lax.all_gather(weight_shard, "dp", axis=0, tiled=True)
    hidden_raw = contract_rows(slot_rows, gathered)
    hidden_grad = (gate_col * hidden_raw).astype(jnp.bfloat16).reshape(activations.shape)
    slot_dgate = jnp.sum(hidden_raw * hidden.astype(jnp.float32), axis=1)
    returned = lax.all_to_all(
        slot_dgate.reshape(peer_count, capacity), "expert", split_axis=0, concat_axis=0, tiled=True
    )
    flat_dgate = jnp.concatenate([returned.reshape(-1), jnp.zeros((1,), jnp.float32)])
    route_dgate = jnp.where(
        is_live, flat_dgate[slot_key].reshape(tok_rows, TOP), jnp.zeros((), jnp.float32)
    )
    mean_term = jnp.sum(route_dgate * affinity, axis=1, keepdims=True) / aff_total
    logit_grad = affinity * (1.0 - affinity) * (2.5 / aff_total) * (route_dgate - mean_term)
    weighted = (gate_col * slot_rows.astype(jnp.float32)).astype(jnp.bfloat16)
    weight_grad = lax.psum_scatter(
        lax.dot_general(
            hidden, weighted, (((0,), (0,)), ((), ())), preferred_element_type=jnp.float32
        ).astype(jnp.bfloat16),
        "dp",
        scatter_dimension=0,
        tiled=True,
    ).astype(jnp.float32)
    return (hidden_grad, weight_grad.reshape(down_weight.shape), logit_grad)


MESH = pl.DeviceIdType.MESH
VMEM_BUDGET = 60 * 1024 * 1024


def flip(index, mask):
    out, bit = index, 1
    while bit <= mask:
        if mask & bit:
            out = out + bit * (1 - 2 * lax.rem(lax.div(index, bit), 2))
        bit *= 2
    return out


def mm(a, b, dims):
    return lax.dot_general(a, b, (dims, ((), ())), preferred_element_type=jnp.float32)


NN, NT = ((1,), (0,)), ((1,), (1,))


def kernel(
    n_dp, n_e, cap, block,
    ids_ref, logit_ref, og_ref, act_ref, w_ref,
    hid_ref, wg_ref, lg_ref,
    packed, rows, actb, act_t, hacc, hsend, hbuf, dsend, drecv,
    a_send, a_recv, y_send, y_recv, s_send, s_recv, f_send, f_recv,
    act_send, act_recv, h_send, h_recv, d_send, d_recv,
):
    me = lax.axis_index("dp")
    ex = lax.axis_index("expert")
    sib, ypart = flip(me, 1), flip(me, 2)
    toks, width = og_ref.shape
    shard = w_ref.shape[0]
    slots = n_e * cap
    half = n_e // 2
    part = half * cap
    blocks = width // block
    my_cols = pl.ds(pl.multiple_of(me * shard, shard), shard)
    group = EXPERTS // n_e

    barrier = pltpu.get_barrier_semaphore()
    for m in range(1, n_e):
        pl.semaphore_signal(barrier, inc=1, device_id={"expert": flip(ex, m)}, device_id_type=MESH)
    for k in range(1, n_dp):
        pl.semaphore_signal(barrier, inc=1, device_id={"dp": flip(me, k)}, device_id_type=MESH)

    ids = ids_ref[0:1, :]
    live = lax.rem(ids, group) == 0
    target = lax.div(ids, group)
    e_iota = lax.broadcasted_iota(jnp.int32, (n_e, toks), 0)
    chosen = jnp.where((target == e_iota) & live, 1.0, 0.0)
    earlier = jnp.where(
        lax.broadcasted_iota(jnp.int32, (toks, toks), 0)
        < lax.broadcasted_iota(jnp.int32, (toks, toks), 1), 1.0, 0.0
    ).astype(jnp.bfloat16)
    before = mm(chosen.astype(jnp.bfloat16), earlier, NN)
    rank = jnp.sum(chosen * before, axis=0, keepdims=True).astype(jnp.int32)
    aff = 1.0 / (1.0 + jnp.exp(-logit_ref[...]))
    total = jnp.sum(aff, axis=0, keepdims=True)
    gate = (2.5 * aff[0:1, :] / total).astype(jnp.bfloat16).astype(jnp.float32)
    slot = jnp.where(live, target * cap + rank, -1)
    s_iota = lax.broadcasted_iota(jnp.int32, (slots, toks), 0)
    place = jnp.where(s_iota == slot, gate, 0.0).astype(jnp.bfloat16)

    def pack(b, carry):
        cols = pl.ds(pl.multiple_of(b * block, block), block)
        got = mm(place, og_ref[:, cols], NN).astype(jnp.bfloat16)
        packed[:, :, cols] = got.reshape(n_e, cap, block)
        return carry

    lax.fori_loop(0, blocks, pack, 0)
    pl.semaphore_wait(barrier, n_e - 1 + n_dp - 1)

    def remote(src, dst, send, recv, where):
        copy = pltpu.make_async_remote_copy(
            src_ref=src, dst_ref=dst, send_sem=send, recv_sem=recv,
            device_id=where, device_id_type=MESH,
        )
        copy.start()
        return copy

    own_copies, y_copies, s_copies, f_copies, sent = {}, {}, {}, {}, []

    def own_step(m):
        src_of = flip(ex, m)
        if m:
            own_copies[m].wait_recv()
        source = packed.at[ex] if m == 0 else rows.at[me, src_of]
        y_copies[m] = remote(source, rows.at[me, src_of], y_send.at[m], y_recv.at[m], {"dp": ypart})
        s_copies[m] = remote(source, rows.at[me, src_of], s_send.at[m], s_recv.at[m], {"dp": sib})

    def y_step(m):
        src_of = flip(ex, m)
        y_copies[m].wait_recv()
        f_copies[m] = remote(
            rows.at[ypart, src_of], rows.at[ypart, src_of], f_send.at[m], f_recv.at[m], {"dp": sib}
        )

    for m in [1] + list(range(half, n_e)) + list(range(2, half)):
        peer = flip(ex, m)
        own_copies[m] = remote(
            packed.at[peer], rows.at[me, ex], a_send.at[m], a_recv.at[m], {"expert": peer}
        )
    own_step(0)
    act_copies = []
    for k in range(1, n_dp):
        peer = flip(me, k)
        theirs = pl.ds(pl.multiple_of(peer * shard, shard), shard)
        act_copies.append(remote(
            act_ref.at[:, theirs], actb.at[me], act_send.at[k], act_recv.at[k], {"dp": peer}
        ))
    rows[me, ex] = packed[ex]
    actb[me] = act_ref[:, my_cols]

    h_copies = {}

    def arrived(g):
        for m in range(g * half, (g + 1) * half):
            s_copies[m].wait_recv()
            f_copies[m].wait_recv()

    def group_start(g):
        first = lax.div(ex, half)
        return (first if g == 0 else 1 - first) * half

    def rows_block(g, cols):
        got = rows[:, pl.ds(group_start(g), half), :, cols]
        return got.reshape(n_dp * part, block)

    def hidden_part(g):
        hacc[...] = jnp.zeros_like(hacc)

        def step(b, carry):
            cols = pl.ds(pl.multiple_of(b * block, block), block)
            hacc[...] += mm(rows_block(g, cols), w_ref[:, cols], NT)
            return carry

        lax.fori_loop(0, blocks, step, 0)
        hsend[g] = hacc[...].astype(jnp.bfloat16).reshape(n_dp, part, shard)
        at = pl.ds(pl.multiple_of(group_start(g) * cap, part), part)
        for k in range(1, n_dp):
            peer = flip(me, k)
            h_copies[g, k] = remote(
                hsend.at[g, peer], hbuf.at[at, my_cols], h_send.at[g, k], h_recv.at[g, k], {"dp": peer}
            )
        hbuf[at, my_cols] = hsend[g, me]

    def grad_part(g):
        at = pl.ds(pl.multiple_of(group_start(g) * cap, part), part)
        act_t[...] = actb[:, at, :].reshape(n_dp * part, shard).T

        def step(b, carry):
            cols = pl.ds(pl.multiple_of(b * block, block), block)
            term = mm(act_t[...], rows_block(g, cols), NN)
            wg_ref[:, cols] = term if g == 0 else wg_ref[:, cols] + term
            return carry

        lax.fori_loop(0, blocks, step, 0)

    lag = 1
    for m in range(1, n_e):
        own_step(m)
        y_step(m - lag)
        if m == half + 1:
            for copy in act_copies:
                copy.wait_recv()
            arrived(0)
            hidden_part(0)
            grad_part(0)
    y_step(n_e - 1)
    arrived(1)
    hidden_part(1)
    grad_part(1)

    for g in range(2):
        for k in range(1, n_dp):
            h_copies[g, k].wait_recv()
    hid_ref[...] = hbuf[...]
    ones = jnp.ones((8, shard), jnp.bfloat16)
    dots = jnp.zeros((8, slots), jnp.float32)
    for j in range(n_dp):
        cols = slice(j * shard, (j + 1) * shard)
        prod = hbuf[:, cols].astype(jnp.float32) * act_ref[:, cols].astype(jnp.float32)
        high = prod.astype(jnp.bfloat16)
        low = (prod - high.astype(jnp.float32)).astype(jnp.bfloat16)
        dots = dots + mm(ones, high, NT) + mm(ones, low, NT)
    dsend[...] = dots[0:1, :]
    d_copies = []
    for m in range(1, n_e):
        d_copies.append(remote(
            dsend, drecv.at[ex], d_send.at[m], d_recv.at[m], {"expert": flip(ex, m)}
        ))
    drecv[ex] = dots[0:1, :]
    pick = jnp.where((s_iota == ex * cap + rank) & live, 1.0, 0.0).astype(jnp.bfloat16)
    for copy in d_copies:
        copy.wait_recv()
    rest = drecv[...].reshape(n_e, slots)
    looked = jnp.zeros((n_e, toks), jnp.float32)
    for _ in range(3):
        piece = rest.astype(jnp.bfloat16)
        looked = looked + mm(piece, pick, NN)
        rest = rest - piece.astype(jnp.float32)
    route = jnp.sum(chosen * looked, axis=0, keepdims=True)
    route = jnp.where(live, route / gate, 0.0)
    mean = route * aff[0:1, :] / total
    k_iota = lax.broadcasted_iota(jnp.int32, aff.shape, 0)
    lg_ref[...] = aff * (1.0 - aff) * (2.5 / total) * (jnp.where(k_iota == 0, route, 0.0) - mean)

    for copies in (own_copies, y_copies, s_copies, f_copies, h_copies):
        for copy in copies.values():
            copy.wait_send()
    for copy in act_copies + d_copies:
        copy.wait_send()


def local(sizes, out_grad, expert_ids, affinity_logits, activations, down_weight):
    n_dp, n_e = sizes["dp"], sizes["expert"]
    toks, width = out_grad.shape
    cap = toks // 16
    slots = n_e * cap
    hidden_width = activations.shape[-1]
    shard = down_weight.shape[1]
    block = 512
    part = slots // 2
    bf16, f32 = jnp.bfloat16, jnp.float32
    row_bytes = 2 * width
    need = (
        toks * row_bytes + slots * row_bytes + n_dp * slots * row_bytes + shard * row_bytes * 3
        + slots * hidden_width * 8 + n_dp * slots * shard * 8 + toks * toks * 8
    )
    fits = (
        n_dp == 4 and n_e >= 4 and n_e & (n_e - 1) == 0 and need < VMEM_BUDGET
        and width % block == 0 and shard % 128 == 0 and (EXPERTS // n_e) % TOP == 0
    )
    if not fits:
        return local_native(out_grad, expert_ids, affinity_logits, activations, down_weight)
    vmem = pl.BlockSpec(memory_space=pltpu.VMEM)
    dma = pltpu.SemaphoreType.DMA
    hidden_grad, weight_grad, logit_t = pl.pallas_call(
        functools.partial(kernel, n_dp, n_e, cap, block),
        out_shape=(
            jax.ShapeDtypeStruct((slots, hidden_width), bf16),
            jax.ShapeDtypeStruct((shard, width), f32),
            jax.ShapeDtypeStruct((TOP, toks), f32),
        ),
        in_specs=[vmem] * 5,
        out_specs=(vmem,) * 3,
        scratch_shapes=[
            pltpu.VMEM((n_e, cap, width), bf16),
            pltpu.VMEM((n_dp, n_e, cap, width), bf16),
            pltpu.VMEM((n_dp, slots, shard), bf16),
            pltpu.VMEM((shard, n_dp * part), bf16),
            pltpu.VMEM((n_dp * part, shard), f32),
            pltpu.VMEM((2, n_dp, part, shard), bf16),
            pltpu.VMEM((slots, hidden_width), bf16),
            pltpu.VMEM((1, slots), f32),
            pltpu.VMEM((n_e, 1, slots), f32),
            dma((n_e,)), dma((n_e,)), dma((n_e,)), dma((n_e,)),
            dma((n_e,)), dma((n_e,)), dma((n_e,)), dma((n_e,)),
            dma((n_dp,)), dma((n_dp,)), dma((2, n_dp)), dma((2, n_dp)),
            dma((n_e,)), dma((n_e,)),
        ],
        compiler_params=pltpu.CompilerParams(
            collective_id=0, has_side_effects=True, vmem_limit_bytes=VMEM_BUDGET
        ),
    )(
        expert_ids.T, affinity_logits.T, out_grad,
        activations.reshape(slots, hidden_width), down_weight[0],
    )
    return (
        hidden_grad.reshape(activations.shape),
        weight_grad.reshape(down_weight.shape),
        logit_t.T,
    )


def solution(mesh):
    return jax.shard_map(
        functools.partial(local, dict(mesh.shape)),
        mesh=mesh,
        in_specs=(
            P(("dp", "expert"), None),
            P(("dp", "expert"), None),
            P(("dp", "expert"), None),
            P("dp", "expert", None, None),
            P("expert", "dp", None),
        ),
        out_specs=(
            P("dp", "expert", None, None),
            P("expert", "dp", None),
            P(("dp", "expert"), None),
        ),
        check_vma=False,
    )
```

```python
import functools

import jax
import jax.numpy as jnp
from jax import lax
from jax.experimental import pallas as pl
from jax.experimental.pallas import tpu as pltpu
from jax.sharding import PartitionSpec as P

EXPERTS = 256
TOP = 8


def contract_rows(slot_rows, weight_rows):
    return lax.dot_general(
        slot_rows, weight_rows, (((1,), (1,)), ((), ())), preferred_element_type=jnp.float32
    )


def local_native(out_grad, expert_ids, affinity_logits, activations, down_weight):
    tok_rows = out_grad.shape[0]
    feat_width = out_grad.shape[1]
    peer_count = lax.axis_size("expert")
    capacity = tok_rows // 16
    slot_count = peer_count * capacity
    group_size = EXPERTS // peer_count
    affinity = jax.nn.sigmoid(affinity_logits)
    aff_total = jnp.sum(affinity, axis=1, keepdims=True)
    gate_vals = 2.5 * affinity / aff_total
    is_live = expert_ids % group_size == 0
    target = expert_ids // group_size
    experts_row = jnp.arange(peer_count, dtype=jnp.int32)[None, None, :]
    onehot = ((target[:, :, None] == experts_row) & is_live[:, :, None]).astype(jnp.int32)
    per_token = jnp.sum(onehot, axis=1)
    before = jnp.cumsum(per_token, axis=0) - per_token
    ranking = jnp.sum(onehot * before[:, None, :], axis=2)
    slot_key = jnp.where(is_live, target * capacity + ranking, slot_count).reshape(-1)
    token_list = jnp.repeat(jnp.arange(tok_rows, dtype=jnp.int32), TOP)
    source_of = (
        jnp.full((slot_count,), tok_rows, jnp.int32).at[slot_key].set(token_list, mode="drop")
    )
    gate_send = (
        jnp.zeros((slot_count,), jnp.float32).at[slot_key].set(gate_vals.reshape(-1), mode="drop")
    )
    gate_send = gate_send.astype(jnp.bfloat16).reshape(peer_count, capacity)
    padded = jnp.concatenate([out_grad, jnp.zeros((1, feat_width), out_grad.dtype)], axis=0)
    send_rows = padded[source_of].reshape(peer_count, capacity, feat_width)
    slot_rows, gate_in = (
        lax.all_to_all(send_rows, "expert", split_axis=0, concat_axis=0, tiled=True),
        lax.all_to_all(gate_send, "expert", split_axis=0, concat_axis=0, tiled=True),
    )
    slot_rows = slot_rows.reshape(slot_count, feat_width)
    gate_col = gate_in.reshape(slot_count, 1).astype(jnp.float32)
    hidden = activations.reshape(slot_count, activations.shape[-1])
    weight_shard = down_weight[0]
    gathered = lax.all_gather(weight_shard, "dp", axis=0, tiled=True)
    hidden_raw = contract_rows(slot_rows, gathered)
    hidden_grad = (gate_col * hidden_raw).astype(jnp.bfloat16).reshape(activations.shape)
    slot_dgate = jnp.sum(hidden_raw * hidden.astype(jnp.float32), axis=1)
    returned = lax.all_to_all(
        slot_dgate.reshape(peer_count, capacity), "expert", split_axis=0, concat_axis=0, tiled=True
    )
    flat_dgate = jnp.concatenate([returned.reshape(-1), jnp.zeros((1,), jnp.float32)])
    route_dgate = jnp.where(
        is_live, flat_dgate[slot_key].reshape(tok_rows, TOP), jnp.zeros((), jnp.float32)
    )
    mean_term = jnp.sum(route_dgate * affinity, axis=1, keepdims=True) / aff_total
    logit_grad = affinity * (1.0 - affinity) * (2.5 / aff_total) * (route_dgate - mean_term)
    weighted = (gate_col * slot_rows.astype(jnp.float32)).astype(jnp.bfloat16)
    weight_grad = lax.psum_scatter(
        lax.dot_general(
            hidden, weighted, (((0,), (0,)), ((), ())), preferred_element_type=jnp.float32
        ).astype(jnp.bfloat16),
        "dp",
        scatter_dimension=0,
        tiled=True,
    ).astype(jnp.float32)
    return (hidden_grad, weight_grad.reshape(down_weight.shape), logit_grad)


MESH = pl.DeviceIdType.MESH
VMEM_ALL = 67043328


def flip(index, mask):
    out, bit = index, 1
    while bit <= mask:
        if mask & bit:
            out = out + bit * (1 - 2 * lax.rem(lax.div(index, bit), 2))
        bit *= 2
    return out


def mm(a, b, dims):
    return lax.dot_general(a, b, (dims, ((), ())), preferred_element_type=jnp.float32)


NN, NT = ((1,), (0,)), ((1,), (1,))


def kernel(
    n_dp, n_e, cap, block,
    ids_ref, logit_ref, og_hbm, act_hbm, w_hbm,
    hid_ref, wg_ref, lg_ref,
    og_ref, act_ref, w_ref, packed, stage, rows, actb, act_t, hacc, hsend, hbuf, dsend, drecv,
    load_sem, w_sem, a_send, a_recv, y_send, y_recv, s_send, s_recv, f_send, f_recv,
    r_send, r_recv, act_send, act_recv, h_send, h_recv, d_send, d_recv,
):
    me = lax.axis_index("dp")
    ex = lax.axis_index("expert")
    sib, ypart = flip(me, 1), flip(me, 2)
    toks, width = og_ref.shape
    shard = w_ref.shape[0]
    slots = n_e * cap
    quarter = n_e // 4
    blocks = width // block
    my_cols = pl.ds(pl.multiple_of(me * shard, shard), shard)
    group = EXPERTS // n_e

    def block_cols(b):
        return pl.ds(pl.multiple_of(b * block, block), block)

    def load(b):
        return pltpu.make_async_copy(
            og_hbm.at[:, block_cols(b)], og_ref.at[:, block_cols(b)], load_sem.at[b]
        )

    for b in range(blocks):
        load(b).start()
    act_load = pltpu.make_async_copy(act_hbm, act_ref, w_sem.at[0])
    act_load.start()
    w_load = pltpu.make_async_copy(w_hbm, w_ref, w_sem.at[1])
    w_load.start()

    barrier = pltpu.get_barrier_semaphore()
    for m in range(1, n_e):
        pl.semaphore_signal(barrier, inc=1, device_id={"expert": flip(ex, m)}, device_id_type=MESH)
    for k in range(1, n_dp):
        pl.semaphore_signal(barrier, inc=1, device_id={"dp": flip(me, k)}, device_id_type=MESH)

    ids = ids_ref[0:1, :]
    live = lax.rem(ids, group) == 0
    target = lax.div(ids, group)
    e_iota = lax.broadcasted_iota(jnp.int32, (n_e, toks), 0)
    chosen = jnp.where((target == e_iota) & live, 1.0, 0.0)
    earlier = jnp.where(
        lax.broadcasted_iota(jnp.int32, (toks, toks), 0)
        < lax.broadcasted_iota(jnp.int32, (toks, toks), 1), 1.0, 0.0
    ).astype(jnp.bfloat16)
    before = mm(chosen.astype(jnp.bfloat16), earlier, NN)
    rank = jnp.sum(chosen * before, axis=0, keepdims=True).astype(jnp.int32)
    aff = 1.0 / (1.0 + jnp.exp(-logit_ref[...]))
    total = jnp.sum(aff, axis=0, keepdims=True)
    gate = (2.5 * aff[0:1, :] / total).astype(jnp.bfloat16).astype(jnp.float32)
    slot = jnp.where(live, target * cap + rank, -1)
    s_iota = lax.broadcasted_iota(jnp.int32, (slots, toks), 0)
    place = jnp.where(s_iota == slot, gate, 0.0).astype(jnp.bfloat16)

    act_load.wait()
    pl.semaphore_wait(barrier, n_e - 1 + n_dp - 1)

    def remote(src, dst, send, recv, where):
        copy = pltpu.make_async_remote_copy(
            src_ref=src, dst_ref=dst, send_sem=send, recv_sem=recv,
            device_id=where, device_id_type=MESH,
        )
        copy.start()
        return copy

    act_copies = []
    for k in range(n_dp - 1, 0, -1):
        peer = flip(me, k)
        theirs = pl.ds(pl.multiple_of(peer * shard, shard), shard)
        act_copies.append(remote(
            act_ref.at[:, theirs], actb.at[me], act_send.at[k], act_recv.at[k], {"dp": peer}
        ))

    def pack(b, carry):
        load(b).wait()
        cols = block_cols(b)
        got = mm(place, og_ref[:, cols], NN).astype(jnp.bfloat16)
        packed[:, :, cols] = got.reshape(n_e, cap, block)
        return carry

    lax.fori_loop(0, blocks, pack, 0)

    quad, low = lax.div(ex, quarter), lax.rem(ex, quarter)
    odd, top = lax.rem(quad, 2), lax.div(quad, 2)
    inner = lax.rem(odd + top, 2)
    across, mirror = quad + 2 - 4 * top, 3 - quad
    quads = [
        quad, quad + 1 - 2 * odd,
        mirror + inner * (across - mirror), across + inner * (mirror - across),
    ]
    kinds = [0, 1, 3 - inner, 2 + inner]

    def source_of(i):
        return quads[i // quarter] * quarter + flip(low, i % quarter)

    own_copies, y_copies, s_copies, f_copies, r_copies, h_copies = {}, {}, {}, {}, {}, {}

    near = 2 * quarter

    def own_step(i):
        src_of = source_of(i)
        if i:
            own_copies[i].wait_recv()
        source = packed.at[ex] if i == 0 else rows.at[me, src_of]
        if i == 0 or i >= near:
            y_copies[i] = remote(source, rows.at[me, src_of], y_send.at[i], y_recv.at[i], {"dp": ypart})
        s_copies[i] = remote(source, rows.at[me, src_of], s_send.at[i], s_recv.at[i], {"dp": sib})

    def relay_step(i):
        y_copies[i].wait_recv()
        r_copies[i] = remote(
            stage.at[i], rows.at[ypart, ex], r_send.at[i], r_recv.at[i], {"expert": source_of(i)}
        )

    def pass_step(i):
        src_of = source_of(i)
        (r_copies if 0 < i < near else y_copies)[i].wait_recv()
        f_copies[i] = remote(
            rows.at[ypart, src_of], rows.at[ypart, src_of], f_send.at[i], f_recv.at[i], {"dp": sib}
        )

    own_step(0)
    for i in range(1, near):
        y_copies[i] = remote(
            packed.at[source_of(i)], stage.at[i], y_send.at[i], y_recv.at[i], {"dp": ypart}
        )
    for i in list(range(1, quarter)) + list(range(near, n_e)) + list(range(quarter, near)):
        peer = source_of(i)
        at = kinds[i // quarter] * quarter + i % quarter
        own_copies[i] = remote(
            packed.at[peer], rows.at[me, ex], a_send.at[at], a_recv.at[at], {"expert": peer}
        )
    rows[me, ex] = packed[ex]
    actb[me] = act_ref[:, my_cols]

    groups = [
        (top * 2 * quarter, 2 * quarter, range(2 * quarter)),
        (quads[2] * quarter, quarter, range(2 * quarter, 3 * quarter)),
        (quads[3] * quarter, quarter, range(3 * quarter, n_e)),
    ]

    def arrived(g):
        for i in groups[g][2]:
            s_copies[i].wait_recv()
            f_copies[i].wait_recv()

    def span(g):
        start, count, _ = groups[g]
        return pl.ds(pl.multiple_of(start * cap, count * cap), count * cap), count * cap

    def rows_block(g, cols):
        start, count, _ = groups[g]
        return rows[:, pl.ds(start, count), :, cols].reshape(n_dp * count * cap, block)

    def hidden_part(g):
        at, extent = span(g)
        acc = hacc.at[pl.ds(0, n_dp * extent)]
        acc[...] = jnp.zeros_like(acc)

        def step(b, carry):
            cols = block_cols(b)
            acc[...] += mm(rows_block(g, cols), w_ref[:, cols], NT)
            return carry

        lax.fori_loop(0, blocks, step, 0)
        hsend[:, at, :] = acc[...].astype(jnp.bfloat16).reshape(n_dp, extent, shard)
        for k in range(n_dp - 1, 0, -1):
            peer = flip(me, k)
            h_copies[g, k] = remote(
                hsend.at[peer, at], hbuf.at[at, my_cols], h_send.at[g, k], h_recv.at[g, k], {"dp": peer}
            )
        hbuf[at, my_cols] = hsend[me, at, :]

    def grad_part(g):
        at, extent = span(g)
        lhs = act_t.at[:, pl.ds(0, n_dp * extent)]
        lhs[...] = actb[:, at, :].reshape(n_dp * extent, shard).T

        def step(b, carry):
            cols = block_cols(b)
            term = mm(lhs[...], rows_block(g, cols), NN)
            wg_ref[:, cols] = term if g == 0 else wg_ref[:, cols] + term
            return carry

        lax.fori_loop(0, blocks, step, 0)

    pass_step(0)
    for i in range(1, near):
        relay_step(i)
    for i in range(1, quarter):
        own_step(i)
    for i in range(near, near + quarter):
        own_step(i)
    for i in range(quarter, near):
        own_step(i)
    for i in range(1, quarter):
        pass_step(i)
    for i in range(near + quarter, n_e):
        own_step(i)
    for i in range(quarter, near + quarter):
        pass_step(i)
    w_load.wait()
    for copy in act_copies:
        copy.wait_recv()
    arrived(0)
    hidden_part(0)
    grad_part(0)
    arrived(1)
    hidden_part(1)
    grad_part(1)
    for i in range(near + quarter, n_e):
        pass_step(i)
    arrived(2)
    hidden_part(2)
    grad_part(2)

    for g in range(3):
        for k in range(1, n_dp):
            h_copies[g, k].wait_recv()
    hid_ref[...] = hbuf[...]
    ones = jnp.ones((8, shard), jnp.bfloat16)
    dots = jnp.zeros((8, slots), jnp.float32)
    for j in range(n_dp):
        cols = slice(j * shard, (j + 1) * shard)
        prod = hbuf[:, cols].astype(jnp.float32) * act_ref[:, cols].astype(jnp.float32)
        high = prod.astype(jnp.bfloat16)
        low = (prod - high.astype(jnp.float32)).astype(jnp.bfloat16)
        dots = dots + mm(ones, high, NT) + mm(ones, low, NT)
    dsend[...] = dots[0:1, :]
    d_copies = []
    for m in range(1, n_e):
        d_copies.append(remote(
            dsend, drecv.at[ex], d_send.at[m], d_recv.at[m], {"expert": flip(ex, m)}
        ))
    drecv[ex] = dots[0:1, :]
    pick = jnp.where((s_iota == ex * cap + rank) & live, 1.0, 0.0).astype(jnp.bfloat16)
    for copy in d_copies:
        copy.wait_recv()
    rest = drecv[...].reshape(n_e, slots)
    looked = jnp.zeros((n_e, toks), jnp.float32)
    for _ in range(3):
        piece = rest.astype(jnp.bfloat16)
        looked = looked + mm(piece, pick, NN)
        rest = rest - piece.astype(jnp.float32)
    route = jnp.sum(chosen * looked, axis=0, keepdims=True)
    route = jnp.where(live, route / gate, 0.0)
    mean = route * aff[0:1, :] / total
    k_iota = lax.broadcasted_iota(jnp.int32, aff.shape, 0)
    lg_ref[...] = aff * (1.0 - aff) * (2.5 / total) * (jnp.where(k_iota == 0, route, 0.0) - mean)

    for copies in (own_copies, y_copies, s_copies, f_copies, r_copies, h_copies):
        for copy in copies.values():
            copy.wait_send()
    for copy in act_copies + d_copies:
        copy.wait_send()


def local(sizes, out_grad, expert_ids, affinity_logits, activations, down_weight):
    n_dp, n_e = sizes["dp"], sizes["expert"]
    toks, width = out_grad.shape
    cap = toks // 16
    slots = n_e * cap
    hidden_width = activations.shape[-1]
    shard = down_weight.shape[1]
    block = 512
    part = slots // 2
    hbm = pl.BlockSpec(memory_space=pltpu.HBM)
    bf16, f32 = jnp.bfloat16, jnp.float32
    row_bytes = 2 * width
    need = (
        toks * row_bytes + 2 * slots * row_bytes + n_dp * slots * row_bytes + shard * row_bytes * 3
        + slots * hidden_width * 8 + n_dp * slots * shard * 8 + toks * toks * 8
    )
    outs = 4 * shard * width + 2 * slots * hidden_width + 4 * TOP * toks
    fits = (
        n_dp == 4 and n_e >= 4 and n_e & (n_e - 1) == 0 and need < VMEM_ALL - 2 * outs
        and width % block == 0 and shard % 128 == 0 and (EXPERTS // n_e) % TOP == 0
    )
    if not fits:
        return local_native(out_grad, expert_ids, affinity_logits, activations, down_weight)
    vmem = pl.BlockSpec(memory_space=pltpu.VMEM)
    dma = pltpu.SemaphoreType.DMA
    hidden_grad, weight_grad, logit_t = pl.pallas_call(
        functools.partial(kernel, n_dp, n_e, cap, block),
        out_shape=(
            pltpu.VMEM((slots, hidden_width), bf16),
            pltpu.VMEM((shard, width), f32),
            pltpu.VMEM((TOP, toks), f32),
        ),
        in_specs=[vmem] * 2 + [hbm] * 3,
        out_specs=(vmem,) * 3,
        scratch_shapes=[
            pltpu.VMEM((toks, width), bf16),
            pltpu.VMEM((slots, hidden_width), bf16),
            pltpu.VMEM((shard, width), bf16),
            pltpu.VMEM((n_e, cap, width), bf16),
            pltpu.VMEM((n_e // 2, cap, width), bf16),
            pltpu.VMEM((n_dp, n_e, cap, width), bf16),
            pltpu.VMEM((n_dp, slots, shard), bf16),
            pltpu.VMEM((shard, n_dp * part), bf16),
            pltpu.VMEM((n_dp * part, shard), f32),
            pltpu.VMEM((n_dp, slots, shard), bf16),
            pltpu.VMEM((slots, hidden_width), bf16),
            pltpu.VMEM((1, slots), f32),
            pltpu.VMEM((n_e, 1, slots), f32),
            dma((width // block,)), dma((2,)),
            dma((n_e,)), dma((n_e,)), dma((n_e,)), dma((n_e,)), dma((n_e,)),
            dma((n_e,)), dma((n_e,)), dma((n_e,)), dma((n_e,)), dma((n_e,)),
            dma((n_dp,)), dma((n_dp,)), dma((3, n_dp)), dma((3, n_dp)),
            dma((n_e,)), dma((n_e,)),
        ],
        compiler_params=pltpu.CompilerParams(
            collective_id=0, has_side_effects=True, vmem_limit_bytes=VMEM_ALL - outs - 128 * 1024
        ),
    )(
        expert_ids.T, affinity_logits.T, out_grad,
        activations.reshape(slots, hidden_width), down_weight[0],
    )
    return (
        hidden_grad.reshape(activations.shape),
        weight_grad.reshape(down_weight.shape),
        logit_t.T,
    )


def solution(mesh):
    return jax.shard_map(
        functools.partial(local, dict(mesh.shape)),
        mesh=mesh,
        in_specs=(
            P(("dp", "expert"), None),
            P(("dp", "expert"), None),
            P(("dp", "expert"), None),
            P("dp", "expert", None, None),
            P("expert", "dp", None),
        ),
        out_specs=(
            P("dp", "expert", None, None),
            P("expert", "dp", None),
            P(("dp", "expert"), None),
        ),
        check_vma=False,
    )
```

```python
import functools

import jax
import jax.numpy as jnp
from jax import lax
from jax.experimental import pallas as pl
from jax.experimental.pallas import tpu as pltpu
from jax.sharding import PartitionSpec as P

EXPERTS = 256
TOP = 8


def contract_rows(slot_rows, weight_rows):
    return lax.dot_general(
        slot_rows, weight_rows, (((1,), (1,)), ((), ())), preferred_element_type=jnp.float32
    )


def local_native(out_grad, expert_ids, affinity_logits, activations, down_weight):
    tok_rows = out_grad.shape[0]
    feat_width = out_grad.shape[1]
    peer_count = lax.axis_size("expert")
    capacity = tok_rows // 16
    slot_count = peer_count * capacity
    group_size = EXPERTS // peer_count
    affinity = jax.nn.sigmoid(affinity_logits)
    aff_total = jnp.sum(affinity, axis=1, keepdims=True)
    gate_vals = 2.5 * affinity / aff_total
    is_live = expert_ids % group_size == 0
    target = expert_ids // group_size
    experts_row = jnp.arange(peer_count, dtype=jnp.int32)[None, None, :]
    onehot = ((target[:, :, None] == experts_row) & is_live[:, :, None]).astype(jnp.int32)
    per_token = jnp.sum(onehot, axis=1)
    before = jnp.cumsum(per_token, axis=0) - per_token
    ranking = jnp.sum(onehot * before[:, None, :], axis=2)
    slot_key = jnp.where(is_live, target * capacity + ranking, slot_count).reshape(-1)
    token_list = jnp.repeat(jnp.arange(tok_rows, dtype=jnp.int32), TOP)
    source_of = (
        jnp.full((slot_count,), tok_rows, jnp.int32).at[slot_key].set(token_list, mode="drop")
    )
    gate_send = (
        jnp.zeros((slot_count,), jnp.float32).at[slot_key].set(gate_vals.reshape(-1), mode="drop")
    )
    gate_send = gate_send.astype(jnp.bfloat16).reshape(peer_count, capacity)
    padded = jnp.concatenate([out_grad, jnp.zeros((1, feat_width), out_grad.dtype)], axis=0)
    send_rows = padded[source_of].reshape(peer_count, capacity, feat_width)
    slot_rows, gate_in = (
        lax.all_to_all(send_rows, "expert", split_axis=0, concat_axis=0, tiled=True),
        lax.all_to_all(gate_send, "expert", split_axis=0, concat_axis=0, tiled=True),
    )
    slot_rows = slot_rows.reshape(slot_count, feat_width)
    gate_col = gate_in.reshape(slot_count, 1).astype(jnp.float32)
    hidden = activations.reshape(slot_count, activations.shape[-1])
    weight_shard = down_weight[0]
    gathered = lax.all_gather(weight_shard, "dp", axis=0, tiled=True)
    hidden_raw = contract_rows(slot_rows, gathered)
    hidden_grad = (gate_col * hidden_raw).astype(jnp.bfloat16).reshape(activations.shape)
    slot_dgate = jnp.sum(hidden_raw * hidden.astype(jnp.float32), axis=1)
    returned = lax.all_to_all(
        slot_dgate.reshape(peer_count, capacity), "expert", split_axis=0, concat_axis=0, tiled=True
    )
    flat_dgate = jnp.concatenate([returned.reshape(-1), jnp.zeros((1,), jnp.float32)])
    route_dgate = jnp.where(
        is_live, flat_dgate[slot_key].reshape(tok_rows, TOP), jnp.zeros((), jnp.float32)
    )
    mean_term = jnp.sum(route_dgate * affinity, axis=1, keepdims=True) / aff_total
    logit_grad = affinity * (1.0 - affinity) * (2.5 / aff_total) * (route_dgate - mean_term)
    weighted = (gate_col * slot_rows.astype(jnp.float32)).astype(jnp.bfloat16)
    weight_grad = lax.psum_scatter(
        lax.dot_general(
            hidden, weighted, (((0,), (0,)), ((), ())), preferred_element_type=jnp.float32
        ).astype(jnp.bfloat16),
        "dp",
        scatter_dimension=0,
        tiled=True,
    ).astype(jnp.float32)
    return (hidden_grad, weight_grad.reshape(down_weight.shape), logit_grad)


MESH = pl.DeviceIdType.MESH
VMEM_ALL = 67043328


def flip(index, mask):
    out, bit = index, 1
    while bit <= mask:
        if mask & bit:
            out = out + bit * (1 - 2 * lax.rem(lax.div(index, bit), 2))
        bit *= 2
    return out


def mm(a, b, dims):
    return lax.dot_general(a, b, (dims, ((), ())), preferred_element_type=jnp.float32)


NN, NT = ((1,), (0,)), ((1,), (1,))


def kernel(
    n_dp, n_e, cap, block,
    ids_ref, logit_ref, og_hbm, act_hbm, w_hbm,
    hid_ref, wg_ref, lg_ref,
    og_ref, act_ref, w_ref, packed, stage, rows, actb, act_t, hacc, hsend, hbuf, dsend, drecv,
    load_sem, w_sem, a_send, a_recv, y_send, y_recv, s_send, s_recv, f_send, f_recv,
    r_send, r_recv, act_send, act_recv, h_send, h_recv, d_send, d_recv,
):
    me = lax.axis_index("dp")
    ex = lax.axis_index("expert")
    sib, ypart = flip(me, 1), flip(me, 2)
    toks, width = og_ref.shape
    shard = w_ref.shape[0]
    slots = n_e * cap
    quarter = n_e // 4
    blocks = width // block
    my_cols = pl.ds(pl.multiple_of(me * shard, shard), shard)
    group = EXPERTS // n_e

    def block_cols(b):
        return pl.ds(pl.multiple_of(b * block, block), block)

    def load(b):
        return pltpu.make_async_copy(
            og_hbm.at[:, block_cols(b)], og_ref.at[:, block_cols(b)], load_sem.at[b]
        )

    for b in range(blocks):
        load(b).start()
    act_load = pltpu.make_async_copy(act_hbm, act_ref, w_sem.at[0])
    act_load.start()
    w_load = pltpu.make_async_copy(w_hbm, w_ref, w_sem.at[1])
    w_load.start()

    barrier = pltpu.get_barrier_semaphore()
    for m in range(1, n_e):
        pl.semaphore_signal(barrier, inc=1, device_id={"expert": flip(ex, m)}, device_id_type=MESH)
    for k in range(1, n_dp):
        pl.semaphore_signal(barrier, inc=1, device_id={"dp": flip(me, k)}, device_id_type=MESH)

    ids = ids_ref[0:1, :]
    live = lax.rem(ids, group) == 0
    target = lax.div(ids, group)
    e_iota = lax.broadcasted_iota(jnp.int32, (n_e, toks), 0)
    chosen = jnp.where((target == e_iota) & live, 1.0, 0.0)
    earlier = jnp.where(
        lax.broadcasted_iota(jnp.int32, (toks, toks), 0)
        < lax.broadcasted_iota(jnp.int32, (toks, toks), 1), 1.0, 0.0
    ).astype(jnp.bfloat16)
    before = mm(chosen.astype(jnp.bfloat16), earlier, NN)
    rank = jnp.sum(chosen * before, axis=0, keepdims=True).astype(jnp.int32)
    aff = 1.0 / (1.0 + jnp.exp(-logit_ref[...]))
    total = jnp.sum(aff, axis=0, keepdims=True)
    gate = (2.5 * aff[0:1, :] / total).astype(jnp.bfloat16).astype(jnp.float32)
    slot = jnp.where(live, target * cap + rank, -1)
    s_iota = lax.broadcasted_iota(jnp.int32, (slots, toks), 0)
    place = jnp.where(s_iota == slot, gate, 0.0).astype(jnp.bfloat16)

    act_load.wait()
    pl.semaphore_wait(barrier, n_e - 1 + n_dp - 1)

    def remote(src, dst, send, recv, where):
        copy = pltpu.make_async_remote_copy(
            src_ref=src, dst_ref=dst, send_sem=send, recv_sem=recv,
            device_id=where, device_id_type=MESH,
        )
        copy.start()
        return copy

    act_copies = []
    for k in range(n_dp - 1, 0, -1):
        peer = flip(me, k)
        theirs = pl.ds(pl.multiple_of(peer * shard, shard), shard)
        act_copies.append(remote(
            act_ref.at[:, theirs], actb.at[me], act_send.at[k], act_recv.at[k], {"dp": peer}
        ))

    def pack(b, carry):
        load(b).wait()
        cols = block_cols(b)
        got = mm(place, og_ref[:, cols], NN).astype(jnp.bfloat16)
        packed[:, :, cols] = got.reshape(n_e, cap, block)
        return carry

    lax.fori_loop(0, blocks, pack, 0)

    quad, low = lax.div(ex, quarter), lax.rem(ex, quarter)
    odd, top = lax.rem(quad, 2), lax.div(quad, 2)
    inner = lax.rem(odd + top, 2)
    across, mirror = quad + 2 - 4 * top, 3 - quad
    quads = [
        quad, quad + 1 - 2 * odd,
        mirror + inner * (across - mirror), across + inner * (mirror - across),
    ]
    kinds = [0, 1, 3 - inner, 2 + inner]

    def source_of(i):
        return quads[i // quarter] * quarter + flip(low, i % quarter)

    own_copies, y_copies, s_copies, f_copies, r_copies, h_copies = {}, {}, {}, {}, {}, {}

    near = 2 * quarter

    def own_step(i):
        src_of = source_of(i)
        if i:
            own_copies[i].wait_recv()
        source = packed.at[ex] if i == 0 else rows.at[me, src_of]
        if i == 0 or i >= quarter:
            y_copies[i] = remote(source, rows.at[me, src_of], y_send.at[i], y_recv.at[i], {"dp": ypart})
        s_copies[i] = remote(source, rows.at[me, src_of], s_send.at[i], s_recv.at[i], {"dp": sib})

    def relay_step(i):
        y_copies[i].wait_recv()
        r_copies[i] = remote(
            stage.at[i], rows.at[ypart, ex], r_send.at[i], r_recv.at[i], {"expert": source_of(i)}
        )

    def pass_step(i):
        src_of = source_of(i)
        (r_copies if 0 < i < quarter else y_copies)[i].wait_recv()
        f_copies[i] = remote(
            rows.at[ypart, src_of], rows.at[ypart, src_of], f_send.at[i], f_recv.at[i], {"dp": sib}
        )

    own_step(0)
    for i in range(1, quarter):
        y_copies[i] = remote(
            packed.at[source_of(i)], stage.at[i], y_send.at[i], y_recv.at[i], {"dp": ypart}
        )
    for i in list(range(1, n_e)):
        peer = source_of(i)
        at = kinds[i // quarter] * quarter + i % quarter
        own_copies[i] = remote(
            packed.at[peer], rows.at[me, ex], a_send.at[at], a_recv.at[at], {"expert": peer}
        )
    rows[me, ex] = packed[ex]
    actb[me] = act_ref[:, my_cols]

    groups = [
        (top * 2 * quarter, 2 * quarter, range(2 * quarter)),
        (quads[2] * quarter, quarter, range(2 * quarter, 3 * quarter)),
        (quads[3] * quarter, quarter, range(3 * quarter, n_e)),
    ]

    def arrived(g):
        for i in groups[g][2]:
            s_copies[i].wait_recv()
            f_copies[i].wait_recv()

    def span(g):
        start, count, _ = groups[g]
        return pl.ds(pl.multiple_of(start * cap, count * cap), count * cap), count * cap

    def rows_block(g, cols):
        start, count, _ = groups[g]
        return rows[:, pl.ds(start, count), :, cols].reshape(n_dp * count * cap, block)

    def hidden_part(g):
        at, extent = span(g)
        acc = hacc.at[pl.ds(0, n_dp * extent)]
        acc[...] = jnp.zeros_like(acc)

        def step(b, carry):
            cols = block_cols(b)
            acc[...] += mm(rows_block(g, cols), w_ref[:, cols], NT)
            return carry

        lax.fori_loop(0, blocks, step, 0)
        hsend[:, at, :] = acc[...].astype(jnp.bfloat16).reshape(n_dp, extent, shard)
        for k in range(n_dp - 1, 0, -1):
            peer = flip(me, k)
            h_copies[g, k] = remote(
                hsend.at[peer, at], hbuf.at[at, my_cols], h_send.at[g, k], h_recv.at[g, k], {"dp": peer}
            )
        hbuf[at, my_cols] = hsend[me, at, :]

    def grad_part(g):
        at, extent = span(g)
        lhs = act_t.at[:, pl.ds(0, n_dp * extent)]
        lhs[...] = actb[:, at, :].reshape(n_dp * extent, shard).T

        def step(b, carry):
            cols = block_cols(b)
            term = mm(lhs[...], rows_block(g, cols), NN)
            wg_ref[:, cols] = term if g == 0 else wg_ref[:, cols] + term
            return carry

        lax.fori_loop(0, blocks, step, 0)

    pass_step(0)
    for i in range(1, quarter):
        relay_step(i)
    for i in range(1, quarter):
        own_step(i)
    for i in range(quarter, near + quarter):
        own_step(i)
    for i in range(1, quarter):
        pass_step(i)
    for i in range(near + quarter, n_e):
        own_step(i)
    for i in range(quarter, near + quarter):
        pass_step(i)
    w_load.wait()
    for copy in act_copies:
        copy.wait_recv()
    arrived(0)
    hidden_part(0)
    grad_part(0)
    arrived(1)
    hidden_part(1)
    grad_part(1)
    for i in range(near + quarter, n_e):
        pass_step(i)
    arrived(2)
    hidden_part(2)
    grad_part(2)

    for g in range(3):
        for k in range(1, n_dp):
            h_copies[g, k].wait_recv()
    hid_ref[...] = hbuf[...]
    ones = jnp.ones((8, shard), jnp.bfloat16)
    dots = jnp.zeros((8, slots), jnp.float32)
    for j in range(n_dp):
        cols = slice(j * shard, (j + 1) * shard)
        prod = hbuf[:, cols].astype(jnp.float32) * act_ref[:, cols].astype(jnp.float32)
        high = prod.astype(jnp.bfloat16)
        low = (prod - high.astype(jnp.float32)).astype(jnp.bfloat16)
        dots = dots + mm(ones, high, NT) + mm(ones, low, NT)
    dsend[...] = dots[0:1, :]
    d_copies = []
    for m in range(1, n_e):
        d_copies.append(remote(
            dsend, drecv.at[ex], d_send.at[m], d_recv.at[m], {"expert": flip(ex, m)}
        ))
    drecv[ex] = dots[0:1, :]
    pick = jnp.where((s_iota == ex * cap + rank) & live, 1.0, 0.0).astype(jnp.bfloat16)
    for copy in d_copies:
        copy.wait_recv()
    rest = drecv[...].reshape(n_e, slots)
    looked = jnp.zeros((n_e, toks), jnp.float32)
    for _ in range(3):
        piece = rest.astype(jnp.bfloat16)
        looked = looked + mm(piece, pick, NN)
        rest = rest - piece.astype(jnp.float32)
    route = jnp.sum(chosen * looked, axis=0, keepdims=True)
    route = jnp.where(live, route / gate, 0.0)
    mean = route * aff[0:1, :] / total
    k_iota = lax.broadcasted_iota(jnp.int32, aff.shape, 0)
    lg_ref[...] = aff * (1.0 - aff) * (2.5 / total) * (jnp.where(k_iota == 0, route, 0.0) - mean)

    for copies in (own_copies, y_copies, s_copies, f_copies, r_copies, h_copies):
        for copy in copies.values():
            copy.wait_send()
    for copy in act_copies + d_copies:
        copy.wait_send()


def local(sizes, out_grad, expert_ids, affinity_logits, activations, down_weight):
    n_dp, n_e = sizes["dp"], sizes["expert"]
    toks, width = out_grad.shape
    cap = toks // 16
    slots = n_e * cap
    hidden_width = activations.shape[-1]
    shard = down_weight.shape[1]
    block = 512
    part = slots // 2
    hbm = pl.BlockSpec(memory_space=pltpu.HBM)
    bf16, f32 = jnp.bfloat16, jnp.float32
    row_bytes = 2 * width
    need = (
        toks * row_bytes + 2 * slots * row_bytes + n_dp * slots * row_bytes + shard * row_bytes * 3
        + slots * hidden_width * 8 + n_dp * slots * shard * 8 + toks * toks * 8
    )
    outs = 4 * shard * width + 2 * slots * hidden_width + 4 * TOP * toks
    fits = (
        n_dp == 4 and n_e >= 4 and n_e & (n_e - 1) == 0 and need < VMEM_ALL - 2 * outs
        and width % block == 0 and shard % 128 == 0 and (EXPERTS // n_e) % TOP == 0
    )
    if not fits:
        return local_native(out_grad, expert_ids, affinity_logits, activations, down_weight)
    vmem = pl.BlockSpec(memory_space=pltpu.VMEM)
    dma = pltpu.SemaphoreType.DMA
    hidden_grad, weight_grad, logit_t = pl.pallas_call(
        functools.partial(kernel, n_dp, n_e, cap, block),
        out_shape=(
            pltpu.VMEM((slots, hidden_width), bf16),
            pltpu.VMEM((shard, width), f32),
            pltpu.VMEM((TOP, toks), f32),
        ),
        in_specs=[vmem] * 2 + [hbm] * 3,
        out_specs=(vmem,) * 3,
        scratch_shapes=[
            pltpu.VMEM((toks, width), bf16),
            pltpu.VMEM((slots, hidden_width), bf16),
            pltpu.VMEM((shard, width), bf16),
            pltpu.VMEM((n_e, cap, width), bf16),
            pltpu.VMEM((n_e // 2, cap, width), bf16),
            pltpu.VMEM((n_dp, n_e, cap, width), bf16),
            pltpu.VMEM((n_dp, slots, shard), bf16),
            pltpu.VMEM((shard, n_dp * part), bf16),
            pltpu.VMEM((n_dp * part, shard), f32),
            pltpu.VMEM((n_dp, slots, shard), bf16),
            pltpu.VMEM((slots, hidden_width), bf16),
            pltpu.VMEM((1, slots), f32),
            pltpu.VMEM((n_e, 1, slots), f32),
            dma((width // block,)), dma((2,)),
            dma((n_e,)), dma((n_e,)), dma((n_e,)), dma((n_e,)), dma((n_e,)),
            dma((n_e,)), dma((n_e,)), dma((n_e,)), dma((n_e,)), dma((n_e,)),
            dma((n_dp,)), dma((n_dp,)), dma((3, n_dp)), dma((3, n_dp)),
            dma((n_e,)), dma((n_e,)),
        ],
        compiler_params=pltpu.CompilerParams(
            collective_id=0, has_side_effects=True, vmem_limit_bytes=VMEM_ALL - outs - 128 * 1024
        ),
    )(
        expert_ids.T, affinity_logits.T, out_grad,
        activations.reshape(slots, hidden_width), down_weight[0],
    )
    return (
        hidden_grad.reshape(activations.shape),
        weight_grad.reshape(down_weight.shape),
        logit_t.T,
    )


def solution(mesh):
    return jax.shard_map(
        functools.partial(local, dict(mesh.shape)),
        mesh=mesh,
        in_specs=(
            P(("dp", "expert"), None),
            P(("dp", "expert"), None),
            P(("dp", "expert"), None),
            P("dp", "expert", None, None),
            P("expert", "dp", None),
        ),
        out_specs=(
            P("dp", "expert", None, None),
            P("expert", "dp", None),
            P(("dp", "expert"), None),
        ),
        check_vma=False,
    )
```
